32 devices in a mesh: row: 4 (over z), col: 8 (over y, x, core).
Axes of the slice: x: 2, y: 2, z: 4, core: 2. Of those that a mesh axis runs over, the one named last changes fastest.
Arguments:
- prior: float32 [4096, 4096], P('row', 'col'), may hold values from -6 to 6, as said below
- observed: int32 [512], replicated, may hold values from 0 to 4095, as said below
- obs_noise: float32 [512], replicated, may hold values from 0.25 to 1
Outputs:
- posterior: float32 [4096, 4096], P('row', 'col')
The draws below stay inside these ranges and needn't reach their ends.
Inputs may be any that keep to these rules, and one draw needn't show every extreme that they name: prior is symmetric positive semidefinite, and exactly symmetric: prior[i, j] equals prior[j, i] bit for bit. States may repeat; the largest and smallest states of the range are observed in every draw.
All inputs are finite; a program needn't handle non-finite values.
Results may differ from the reference program's by a relative error of at most 0.00012.
Values sent between devices are 32-bit elements; how exact they have to be, the bound alone decides.
A program may use at most 128 MiB of HBM per device.

```python
import math
import jax
import jax.numpy as jnp
from jax import lax

M = 512
RANK = 1024
N = 4096


def draw_prior(key, part):
    factor = jnp.clip(jax.random.normal(key, (N, RANK), jnp.float32), -4.0, 4.0)
    product = jnp.dot(factor, factor.T, precision=lax.Precision.HIGHEST, preferred_element_type=jnp.float32) / RANK
    return ((product + product.T) * 0.5).astype(jnp.float32)


def draw_observed(key, part):
    states = jax.random.randint(key, (M,), 0, N)
    first = jax.random.randint(jax.random.fold_in(key, 11), (), 0, M)
    offset = jax.random.randint(jax.random.fold_in(key, 12), (), 1, M)
    second = (first + offset) % M
    places = jnp.arange(M)
    states = jnp.where(places == first, N - 1, states)
    states = jnp.where(places == second, 0, states)
    return states.astype(jnp.int32)


def setup_inputs(seed: int = 0) -> dict:
    key_of = jax.random.split(jax.random.key(seed), 4)
    prior = draw_prior(jax.random.fold_in(key_of[3], 71), 0)
    observed = draw_observed(jax.random.fold_in(key_of[3], 71), 0)
    obs_noise = jnp.clip(jnp.exp(jax.random.uniform(key_of[2], (M,), jnp.float32, math.log(0.25), math.log(1.0))), 0.25, 1.0)
    return {"prior": prior, "observed": observed, "obs_noise": obs_noise}


def reference(prior, observed, obs_noise):
    panel = jnp.take(prior, observed, axis=1)
    innovation = jnp.take(panel, observed, axis=0) + jnp.diag(obs_noise)
    factor = jnp.linalg.cholesky(innovation)
    forward = lax.linalg.triangular_solve(factor, panel.T, left_side=True, lower=True)
    weighted = lax.linalg.triangular_solve(factor, forward, left_side=True, lower=True, transpose_a=True)
    update = lax.dot_general(weighted.astype(jnp.float32), panel.astype(jnp.float32), (((0,), (1,)), ((), ())), precision=lax.Precision.HIGHEST, preferred_element_type=jnp.float32)
    return prior - update.T
```

```python
import functools

import jax
import jax.numpy as jnp
from jax import lax
from jax.experimental import pallas as pl
from jax.experimental.pallas import tpu as pltpu
from jax.sharding import PartitionSpec as P

F32 = jnp.float32
BF16 = jnp.bfloat16
HI = lax.Precision.HIGHEST
MESH = pl.DeviceIdType.MESH
VMEM = pl.BlockSpec(memory_space=pltpu.VMEM)
LIMIT = 60 * 1024 * 1024


def parts3(x):
    first = x.astype(BF16)
    rest = x - first.astype(F32)
    second = rest.astype(BF16)
    third = (rest - second.astype(F32)).astype(BF16)
    return first, second, third


def dot(a, b):
    return jnp.dot(a, b, preferred_element_type=F32)


def pick_kernel(prior_ref, obs_col_ref, obs_row_ref, s_ref, a_ref, b_ref, one_ref):
    rows, cols = prior_ref.shape
    obs = obs_row_ref.shape[1]
    row_start = lax.axis_index("row") * rows
    col_start = lax.axis_index("col") * cols
    in_cols = lax.broadcasted_iota(jnp.int32, (cols, obs), 0) == obs_row_ref[...] - col_start
    one_ref[...] = jnp.where(in_cols, 1.0, 0.0).astype(BF16)
    tile = 256

    @pl.loop(0, rows // tile)
    def _(t):
        at = pl.ds(pl.multiple_of(t * tile, tile), tile)
        block = prior_ref[at, :]
        p1, p2, p3 = parts3(block)
        pick = one_ref[...]
        a_ref[at, :] = dot(p1, pick) + dot(p2, pick) + dot(p3, pick)
        local = obs_col_ref[...] - (row_start + t * tile)
        left = (lax.broadcasted_iota(jnp.int32, (obs, tile), 1) == local)
        left = jnp.where(left, 1.0, 0.0).astype(BF16)
        got = dot(left, p1) + dot(left, p2) + dot(left, p3)

        @pl.when(t == 0)
        def _():
            b_ref[...] = got

        @pl.when(t > 0)
        def _():
            b_ref[...] += got

    half = obs // 2

    @pl.loop(0, 2)
    def _(t):
        at = pl.ds(pl.multiple_of(t * half, half), half)
        g1, g2, g3 = parts3(b_ref[at, :])
        pick = one_ref[...]
        s_ref[at, :] = dot(g1, pick) + dot(g2, pick) + dot(g3, pick)


def pick_local(prior, observed):
    rows, cols = prior.shape
    obs = observed.shape[0]
    return pl.pallas_call(
        pick_kernel,
        name="pick_local",
        out_shape=(
            jax.ShapeDtypeStruct((obs, obs), F32),
            jax.ShapeDtypeStruct((rows, obs), F32),
            jax.ShapeDtypeStruct((obs, cols), F32),
        ),
        in_specs=[VMEM] * 3,
        out_specs=(VMEM,) * 3,
        scratch_shapes=[pltpu.VMEM((cols, obs), BF16)],
        compiler_params=pltpu.CompilerParams(vmem_limit_bytes=LIMIT),
    )(prior, observed[:, None], observed[None, :])


def bits(size):
    return list(range(size.bit_length() - 1))


def partner(axis, bit):
    me = lax.axis_index(axis)
    one = (me // (1 << bit)) % 2
    return one, {axis: me + (1 - 2 * one) * (1 << bit)}


def greet(axes):
    barrier = pltpu.get_barrier_semaphore()
    for axis, bit in axes:
        _, peer = partner(axis, bit)
        pl.semaphore_signal(barrier, inc=1, device_id=peer, device_id_type=MESH)
    pl.semaphore_wait(barrier, len(axes))


def phases(src, out, acc, recv, send_sem, recv_sem, first_sem, rows, lanes, halving, whole):
    lane = pl.ds(lanes[0], lanes[1])
    state = {"off": 0, "n": rows, "live": src, "path": []}
    result = []
    sem = first_sem

    def at(off, n):
        return pl.ds(pl.multiple_of(off, 8), n)

    for index, (axis, bit) in enumerate(halving):
        def start(axis=axis, bit=bit, index=index, sem=sem):
            one, peer = partner(axis, bit)
            n = state["n"] // 2
            keep = state["off"] + one * n
            give = state["off"] + (1 - one) * n
            copy = pltpu.make_async_remote_copy(
                state["live"].at[at(give, n), lane], recv[index], send_sem.at[sem], recv_sem.at[sem],
                device_id=peer, device_id_type=MESH)
            copy.start()
            state["path"].append((keep, n, peer))
            state["off"], state["n"], state["copy"] = keep, n, copy

        def finish(index=index):
            state["copy"].wait()
            where = at(state["off"], state["n"])
            acc[where, lane] = state["live"][where, lane] + recv[index][...]
            state["live"] = acc

        result.append((start, finish))
        sem += 1
    for index, (axis, bit) in enumerate(whole):
        def start(axis=axis, bit=bit, index=index, sem=sem):
            _, peer = partner(axis, bit)
            where = at(state["off"], state["n"])
            copy = pltpu.make_async_remote_copy(
                acc.at[where, lane], recv[len(halving) + index], send_sem.at[sem], recv_sem.at[sem],
                device_id=peer, device_id_type=MESH)
            copy.start()
            state["copy"] = copy

        def finish(index=index):
            state["copy"].wait()
            where = at(state["off"], state["n"])
            acc[where, lane] = acc[where, lane] + recv[len(halving) + index][...]

        result.append((start, finish))
        sem += 1
    for index in range(len(halving)):
        def start(index=index, sem=sem):
            keep, n, peer = state["path"][len(halving) - 1 - index]
            where = at(keep, n)
            if index == 0:
                out[where, lane] = acc[where, lane]
            copy = pltpu.make_async_remote_copy(
                out.at[where, lane], out.at[where, lane], send_sem.at[sem], recv_sem.at[sem],
                device_id=peer, device_id_type=MESH)
            copy.start()
            state["copy"] = copy

        def finish():
            state["copy"].wait()

        result.append((start, finish))
        sem += 1
    return result


def orders(col_bits):
    return [col_bits, col_bits[:1] + col_bits[1:][::-1]]


def recv_shapes(rows, width, halving, whole):
    shapes = []
    for _ in range(halving):
        rows //= 2
        shapes.append(pltpu.VMEM((rows, width), F32))
    return shapes + [pltpu.VMEM((rows, width), F32)] * whole


def innovation_kernel(col_bits, row_bits, part_ref, out_ref, acc, *rest):
    send_sem, recv_sem = rest[-2:]
    bufs = rest[:-2]
    obs = part_ref.shape[0]
    streams = orders(col_bits)
    width = obs // len(streams)
    each = len(bufs) // len(streams)
    steps = 2 * len(col_bits) + len(row_bits)
    greet([("col", b) for b in col_bits] + [("row", b) for b in row_bits])
    plans = [
        phases(part_ref, out_ref, acc, bufs[i * each:(i + 1) * each], send_sem, recv_sem, i * steps, obs,
               (i * width, width), [("col", b) for b in order], [("row", b) for b in row_bits])
        for i, order in enumerate(streams)
    ]
    for step in range(steps):
        for plan in plans:
            plan[step][0]()
        for plan in plans:
            plan[step][1]()


def reduce_innovation(part, mesh):
    obs = part.shape[0]
    col_bits, row_bits = bits(mesh.shape["col"]), bits(mesh.shape["row"])
    steps = 2 * len(col_bits) + len(row_bits)
    return pl.pallas_call(
        functools.partial(innovation_kernel, col_bits, row_bits),
        name="reduce_innovation",
        out_shape=jax.ShapeDtypeStruct((obs, obs), F32),
        in_specs=[VMEM],
        out_specs=VMEM,
        scratch_shapes=[pltpu.VMEM((obs, obs), F32)]
        + recv_shapes(obs, obs // 2, len(col_bits), len(row_bits)) * 2
        + [pltpu.SemaphoreType.DMA((2 * steps,)), pltpu.SemaphoreType.DMA((2 * steps,))],
        compiler_params=pltpu.CompilerParams(collective_id=0, has_side_effects=True, vmem_limit_bytes=LIMIT),
    )(part)


def row_of(x, k):
    return jnp.broadcast_to(x[k:k + 1, :], x.shape)


def factor_block(d, m):
    size = d.shape[0]
    sub = lax.broadcasted_iota(jnp.int32, (8, size), 0)
    lane = lax.broadcasted_iota(jnp.int32, (8, size), 1)
    done = []
    for mb in range(size // 8):
        panel, right = d[:8], m[:8]
        cols = [jnp.broadcast_to(panel[:, 8 * mb + j:8 * mb + j + 1], (8, size)) for j in range(8)]
        for k in range(8):
            inv = lax.rsqrt(row_of(cols[k], k))
            low = jnp.where(sub > k, cols[k] * inv, 0.0)
            up, um = row_of(panel, k) * inv, row_of(right, k) * inv
            panel = jnp.where(sub == k, up, panel - low * up)
            right = jnp.where(sub == k, um, right - low * um)
            for j in range(k + 1, 8):
                cols[j] = cols[j] - low * row_of(low, j)
        done.append(right)
        if mb + 1 < size // 8:
            both = jnp.concatenate([panel, right], axis=1)
            step = lax.dot_general(panel, both, (((0,), (0,)), ((), ())), precision=HI, preferred_element_type=F32)
            step = step[8 * (mb + 1):]
            d = d[8:] - step[:, :size]
            m = m[8:] - step[:, size:]
    return jnp.concatenate(done, axis=0)


def factor_kernel(s_ref, noise_ref, inv_ref, sm):
    obs = s_ref.shape[0]
    nb = 128
    i = lax.broadcasted_iota(jnp.int32, (obs, obs), 0)
    j = lax.broadcasted_iota(jnp.int32, (obs, obs), 1)
    sm[:, :obs] = s_ref[...] + jnp.where(i == j, noise_ref[...], 0.0)
    sm[:, obs:] = jnp.where(i == j, 1.0, 0.0)
    eye = jnp.where(i[:nb, :nb] == j[:nb, :nb], 1.0, 0.0).astype(F32)
    wide = lax.broadcasted_iota(jnp.int32, (nb, obs), 1)

    @pl.loop(0, obs // nb)
    def _(kb):
        at = pl.ds(pl.multiple_of(kb * nb, nb), nb)
        linv = factor_block(sm[at, at], eye)
        row = jnp.dot(linv, sm[at, :], precision=HI, preferred_element_type=F32)
        inv_ref[at, :] = row[:, obs:]
        below = jnp.where(wide >= (kb + 1) * nb, row[:, :obs], 0.0)
        sm[...] -= lax.dot_general(below, row, (((0,), (0,)), ((), ())), precision=HI, preferred_element_type=F32)


def factor_inverse(s, noise):
    obs = s.shape[0]
    return pl.pallas_call(
        factor_kernel,
        name="factor_inverse",
        out_shape=jax.ShapeDtypeStruct((obs, obs), F32),
        in_specs=[VMEM, VMEM],
        out_specs=VMEM,
        scratch_shapes=[pltpu.VMEM((obs, 2 * obs), F32)],
        compiler_params=pltpu.CompilerParams(vmem_limit_bytes=LIMIT),
        cost_estimate=pl.CostEstimate(flops=4 * obs * obs * obs, bytes_accessed=obs * obs * 8, transcendentals=obs),
    )(s, noise[None, :])


def local(mesh, prior, observed, obs_noise):
    s_part, a_part, b_part = pick_local(prior, observed)
    s = reduce_innovation(s_part, mesh)
    a = lax.psum(a_part, "col")
    b = lax.psum(b_part, "row")
    linv = factor_inverse(s, obs_noise)
    v = jnp.dot(linv, b, precision=HI, preferred_element_type=F32)
    y = jnp.dot(linv.T, v, precision=HI, preferred_element_type=F32)
    return prior - jnp.dot(a, y, precision=HI, preferred_element_type=F32)


def solution(mesh):
    return jax.shard_map(
        functools.partial(local, mesh),
        mesh=mesh,
        in_specs=(P("row", "col"), P(), P()),
        out_specs=P("row", "col"),
        check_vma=False,
    )
```

```python
import functools

import jax
import jax.numpy as jnp
from jax import lax
from jax.experimental import pallas as pl
from jax.experimental.pallas import tpu as pltpu
from jax.sharding import PartitionSpec as P

F32 = jnp.float32
BF16 = jnp.bfloat16
HI = lax.Precision.HIGHEST
MID = lax.Precision.HIGH
MESH = pl.DeviceIdType.MESH
VMEM = pl.BlockSpec(memory_space=pltpu.VMEM)
LIMIT = 60 * 1024 * 1024


def parts3(x):
    first = x.astype(BF16)
    rest = x - first.astype(F32)
    second = rest.astype(BF16)
    third = (rest - second.astype(F32)).astype(BF16)
    return first, second, third


def dot(a, b):
    return jnp.dot(a, b, preferred_element_type=F32)


def pick_kernel(prior_ref, obs_col_ref, obs_row_ref, s_ref, a_ref, b_ref, one_ref):
    rows, cols = prior_ref.shape
    obs = obs_row_ref.shape[1]
    row_start = lax.axis_index("row") * rows
    col_start = lax.axis_index("col") * cols
    in_cols = lax.broadcasted_iota(jnp.int32, (cols, obs), 0) == obs_row_ref[...] - col_start
    one_ref[...] = jnp.where(in_cols, 1.0, 0.0).astype(BF16)
    tile = 256

    @pl.loop(0, rows // tile)
    def _(t):
        at = pl.ds(pl.multiple_of(t * tile, tile), tile)
        block = prior_ref[at, :]
        p1, p2, p3 = parts3(block)
        pick = one_ref[...]
        a_ref[at, :] = dot(p1, pick) + dot(p2, pick) + dot(p3, pick)
        local = obs_col_ref[...] - (row_start + t * tile)
        left = (lax.broadcasted_iota(jnp.int32, (obs, tile), 1) == local)
        left = jnp.where(left, 1.0, 0.0).astype(BF16)
        got = dot(left, p1) + dot(left, p2) + dot(left, p3)

        @pl.when(t == 0)
        def _():
            b_ref[...] = got

        @pl.when(t > 0)
        def _():
            b_ref[...] += got

    half = obs // 2

    @pl.loop(0, 2)
    def _(t):
        at = pl.ds(pl.multiple_of(t * half, half), half)
        g1, g2, g3 = parts3(b_ref[at, :])
        pick = one_ref[...]
        s_ref[at, :] = dot(g1, pick) + dot(g2, pick) + dot(g3, pick)


def pick_local(prior, observed):
    rows, cols = prior.shape
    obs = observed.shape[0]
    return pl.pallas_call(
        pick_kernel,
        name="pick_local",
        out_shape=(
            jax.ShapeDtypeStruct((obs, obs), F32),
            jax.ShapeDtypeStruct((rows, obs), F32),
            jax.ShapeDtypeStruct((obs, cols), F32),
        ),
        in_specs=[VMEM] * 3,
        out_specs=(VMEM,) * 3,
        scratch_shapes=[pltpu.VMEM((cols, obs), BF16)],
        compiler_params=pltpu.CompilerParams(vmem_limit_bytes=LIMIT),
    )(prior, observed[:, None], observed[None, :])


def bits(size):
    return list(range(size.bit_length() - 1))


def partner(axis, bit):
    me = lax.axis_index(axis)
    one = (me // (1 << bit)) % 2
    return one, {axis: me + (1 - 2 * one) * (1 << bit)}


def greet(axes):
    barrier = pltpu.get_barrier_semaphore()
    for axis, bit in axes:
        _, peer = partner(axis, bit)
        pl.semaphore_signal(barrier, inc=1, device_id=peer, device_id_type=MESH)
    pl.semaphore_wait(barrier, len(axes))


def phases(src, out, acc, recv, send_sem, recv_sem, first_sem, lanes, halving, whole):
    lane = pl.ds(lanes[0], lanes[1])
    off, n, live = 0, src.shape[0], src
    result, path = [], []

    def at(off, n):
        return pl.ds(pl.multiple_of(off, 8), n)

    def send(source, target, peer):
        sem = first_sem + len(result)
        return pltpu.make_async_remote_copy(
            source, target, send_sem.at[sem], recv_sem.at[sem], device_id=peer, device_id_type=MESH)

    def reducing(copy, where, live, buf):
        def finish():
            copy.wait()
            acc[where, lane] = live[where, lane] + buf[...]

        result.append((copy.start, finish))

    for axis, bit in halving:
        one, peer = partner(axis, bit)
        n //= 2
        give = at(off + (1 - one) * n, n)
        off = off + one * n
        buf = recv[len(result)]
        reducing(send(live.at[give, lane], buf, peer), at(off, n), live, buf)
        live = acc
        path.append((off, n, peer))
    for axis, bit in whole:
        _, peer = partner(axis, bit)
        buf = recv[len(result)]
        where = at(off, n)
        reducing(send(acc.at[where, lane], buf, peer), where, acc, buf)
    for index, (off, n, peer) in enumerate(path[::-1]):
        where = at(off, n)
        copy = send(out.at[where, lane], out.at[where, lane], peer)

        def start(copy=copy, where=where, first=index == 0):
            if first:
                out[where, lane] = acc[where, lane]
            copy.start()

        result.append((start, copy.wait))
    return result


def orders(col_bits):
    return [col_bits, col_bits[:1] + col_bits[1:][::-1]]


def recv_shapes(rows, width, halving, whole):
    shapes = []
    for _ in range(halving):
        rows //= 2
        shapes.append(pltpu.VMEM((rows, width), F32))
    return shapes + [pltpu.VMEM((rows, width), F32)] * whole


def row_of(x, k):
    return jnp.broadcast_to(x[k:k + 1, :], x.shape)


def factor_block(d, m, tick):
    size = d.shape[0]
    sub = lax.broadcasted_iota(jnp.int32, (8, size), 0)
    lane = lax.broadcasted_iota(jnp.int32, (8, size), 1)
    done = []
    for mb in range(size // 8):
        tick(mb)
        panel, right = d[:8], m[:8]
        cols = [jnp.broadcast_to(panel[:, 8 * mb + j:8 * mb + j + 1], (8, size)) for j in range(8)]
        for k in range(8):
            inv = lax.rsqrt(row_of(cols[k], k))
            low = jnp.where(sub > k, cols[k] * inv, 0.0)
            up, um = row_of(panel, k) * inv, row_of(right, k) * inv
            panel = jnp.where(sub == k, up, panel - low * up)
            right = jnp.where(sub == k, um, right - low * um)
            for j in range(k + 1, 8):
                cols[j] = cols[j] - low * row_of(low, j)
        done.append(right)
        if mb + 1 < size // 8:
            both = jnp.concatenate([panel, right], axis=1)
            step = lax.dot_general(panel, both, (((0,), (0,)), ((), ())), precision=HI, preferred_element_type=F32)
            step = step[8 * (mb + 1):]
            d = d[8:] - step[:, :size]
            m = m[8:] - step[:, size:]
    return jnp.concatenate(done, axis=0)


NB = 128
TICKS = 4


def update_kernel(col_bits, row_bits, s_part, a_part, b_part, noise_ref, inv_ref, a_ref, b_ref, s_ref, sm, *rest):
    send_sem, recv_sem = rest[-2:]
    (s_acc, a_acc, b_acc), bufs = rest[:3], list(rest[3:-2])
    obs = s_part.shape[0]
    col_axes = [[("col", b) for b in order] for order in orders(col_bits)]
    row_axes = [("row", b) for b in row_bits]
    greet(col_axes[0] + row_axes)
    sems = [0]

    def plan(src, out, acc, lanes, halving, whole):
        count = len(halving) + len(whole)
        mine = [bufs.pop(0) for _ in range(count)]
        steps = phases(src, out, acc, mine, send_sem, recv_sem, sems[0], lanes, halving, whole)
        sems[0] += len(steps)
        return steps

    width = obs // 2
    s_plans = [plan(s_part, s_ref, s_acc, (i * width, width), col_axes[i], row_axes) for i in range(2)]
    a_plans = [plan(a_part, a_ref, a_acc, (i * width, width), col_axes[i], []) for i in range(2)]
    b_plan = plan(b_part, b_ref, b_acc, (0, b_part.shape[1]), row_axes, [])

    for step in range(len(s_plans[0])):
        for steps in s_plans:
            steps[step][0]()
        if step == len(col_bits) + len(row_bits):
            b_plan[0][0]()
        for steps in s_plans:
            steps[step][1]()

    total = TICKS * (obs // NB)
    actions = [[] for _ in range(total + 1)]
    for steps, span, begun in [(a_plans[0], total, False), (a_plans[1], total, False), (b_plan, total - 1, True)]:
        if not begun:
            actions[0].append(steps[0][0])
        for index in range(len(steps)):
            slot = actions[round(span * (index + 1) / len(steps))]
            slot.append(steps[index][1])
            if index + 1 < len(steps):
                slot.append(steps[index + 1][0])

    i = lax.broadcasted_iota(jnp.int32, (obs, obs), 0)
    j = lax.broadcasted_iota(jnp.int32, (obs, obs), 1)
    sm[:, :obs] = s_ref[...] + jnp.where(i == j, noise_ref[...], 0.0)
    sm[:, obs:] = jnp.where(i == j, 1.0, 0.0)
    eye = jnp.where(i[:NB, :NB] == j[:NB, :NB], 1.0, 0.0).astype(F32)
    wide = lax.broadcasted_iota(jnp.int32, (NB, obs), 1)

    @pl.loop(0, obs // NB)
    def _(kb):
        def tick(mb):
            if mb % (NB // 8 // TICKS):
                return
            for block in range(obs // NB):
                todo = actions[block * TICKS + mb // (NB // 8 // TICKS)]
                if todo:
                    @pl.when(kb == block)
                    def _():
                        for act in todo:
                            act()

        at = pl.ds(pl.multiple_of(kb * NB, NB), NB)
        linv = factor_block(sm[at, at], eye, tick)
        row = jnp.dot(linv, sm[at, :], precision=HI, preferred_element_type=F32)
        inv_ref[at, :] = row[:, obs:]
        below = jnp.where(wide >= (kb + 1) * NB, row[:, :obs], 0.0)
        sm[...] -= lax.dot_general(below, row, (((0,), (0,)), ((), ())), precision=HI, preferred_element_type=F32)

    for act in actions[total]:
        act()


def update_parts(s_part, a_part, b_part, noise, mesh):
    obs = s_part.shape[0]
    col_bits, row_bits = bits(mesh.shape["col"]), bits(mesh.shape["row"])
    nc, nr = len(col_bits), len(row_bits)
    copies = 2 * (2 * nc + nr) + 2 * 2 * nc + 2 * nr
    like = jax.ShapeDtypeStruct
    return pl.pallas_call(
        functools.partial(update_kernel, col_bits, row_bits),
        name="update_parts",
        out_shape=(like((obs, obs), F32), like(a_part.shape, F32), like(b_part.shape, F32)),
        in_specs=[VMEM] * 4,
        out_specs=(VMEM,) * 3,
        scratch_shapes=[
            pltpu.VMEM((obs, obs), F32),
            pltpu.VMEM((obs, 2 * obs), F32),
            pltpu.VMEM(s_part.shape, F32),
            pltpu.VMEM(a_part.shape, F32),
            pltpu.VMEM(b_part.shape, F32),
        ]
        + recv_shapes(obs, obs // 2, nc, nr) * 2
        + recv_shapes(a_part.shape[0], obs // 2, nc, 0) * 2
        + recv_shapes(obs, b_part.shape[1], nr, 0)
        + [pltpu.SemaphoreType.DMA((copies,)), pltpu.SemaphoreType.DMA((copies,))],
        compiler_params=pltpu.CompilerParams(collective_id=0, has_side_effects=True, vmem_limit_bytes=LIMIT),
    )(s_part, a_part, b_part, noise[None, :])


def local(mesh, prior, observed, obs_noise):
    s_part, a_part, b_part = pick_local(prior, observed)
    linv, a, b = update_parts(s_part, a_part, b_part, obs_noise, mesh)
    v = jnp.dot(linv, b, precision=MID, preferred_element_type=F32)
    y = jnp.dot(linv.T, v, precision=MID, preferred_element_type=F32)
    return prior - jnp.dot(a, y, precision=MID, preferred_element_type=F32)


def solution(mesh):
    return jax.shard_map(
        functools.partial(local, mesh),
        mesh=mesh,
        in_specs=(P("row", "col"), P(), P()),
        out_specs=P("row", "col"),
        check_vma=False,
    )
```

```python
import functools

import jax
import jax.numpy as jnp
from jax import lax
from jax.experimental import pallas as pl
from jax.experimental.pallas import tpu as pltpu
from jax.sharding import PartitionSpec as P

F32 = jnp.float32
BF16 = jnp.bfloat16
HI = lax.Precision.HIGHEST
MID = lax.Precision.HIGH
MESH = pl.DeviceIdType.MESH
VMEM = pl.BlockSpec(memory_space=pltpu.VMEM)
LIMIT = 60 * 1024 * 1024


def parts3(x):
    first = x.astype(BF16)
    rest = x - first.astype(F32)
    second = rest.astype(BF16)
    third = (rest - second.astype(F32)).astype(BF16)
    return first, second, third


def dot(a, b):
    return jnp.dot(a, b, preferred_element_type=F32)


TILE = 256


def pick_rows(prior_ref, obs_ref, one_ref, s_ref, b_ref):
    rows, cols = prior_ref.shape
    obs = obs_ref.shape[1]
    row_start = lax.axis_index("row") * rows
    col_start = lax.axis_index("col") * cols
    in_cols = lax.broadcasted_iota(jnp.int32, (cols, obs), 0) == obs_ref[...] - col_start
    one_ref[...] = jnp.where(in_cols, 1.0, 0.0).astype(BF16)
    tall = jnp.broadcast_to(obs_ref[...].astype(F32), (8, obs)).T[:, :1].astype(jnp.int32)

    @pl.loop(0, rows // TILE)
    def _(t):
        at = pl.ds(pl.multiple_of(t * TILE, TILE), TILE)
        p1, p2, p3 = parts3(prior_ref[at, :])
        left = lax.broadcasted_iota(jnp.int32, (obs, TILE), 1) == tall - (row_start + t * TILE)
        left = jnp.where(left, 1.0, 0.0).astype(BF16)
        got = dot(left, p1) + dot(left, p2) + dot(left, p3)

        @pl.when(t == 0)
        def _():
            b_ref[...] = got

        @pl.when(t > 0)
        def _():
            b_ref[...] += got

    @pl.loop(0, obs // TILE)
    def _(t):
        at = pl.ds(pl.multiple_of(t * TILE, TILE), TILE)
        g1, g2, g3 = parts3(b_ref[at, :])
        pick = one_ref[...]
        s_ref[at, :] = dot(g1, pick) + dot(g2, pick) + dot(g3, pick)


def pick_columns(prior_ref, one_ref, a_ref, first, last):
    @pl.loop(first, last)
    def _(t):
        at = pl.ds(pl.multiple_of(t * TILE, TILE), TILE)
        p1, p2, p3 = parts3(prior_ref[at, :])
        pick = one_ref[...]
        a_ref[at, :] = dot(p1, pick) + dot(p2, pick) + dot(p3, pick)


def bits(size):
    return list(range(size.bit_length() - 1))


def partner(axis, bit):
    me = lax.axis_index(axis)
    one = (me // (1 << bit)) % 2
    return one, {axis: me + (1 - 2 * one) * (1 << bit)}


def greet(axes):
    barrier = pltpu.get_barrier_semaphore()
    for axis, bit in axes:
        _, peer = partner(axis, bit)
        pl.semaphore_signal(barrier, inc=1, device_id=peer, device_id_type=MESH)
    pl.semaphore_wait(barrier, len(axes))


def phases(src, out, acc, recv, send_sem, recv_sem, first_sem, lanes, halving, whole):
    lane = pl.ds(lanes[0], lanes[1])
    off, n, live = 0, src.shape[0], src
    result, path = [], []

    def at(off, n):
        return pl.ds(pl.multiple_of(off, 8), n)

    def send(source, target, peer):
        sem = first_sem + len(result)
        return pltpu.make_async_remote_copy(
            source, target, send_sem.at[sem], recv_sem.at[sem], device_id=peer, device_id_type=MESH)

    def reducing(copy, where, live, buf):
        def finish():
            copy.wait()
            acc[where, lane] = live[where, lane] + buf[...]

        result.append((copy.start, finish))

    for axis, bit in halving:
        one, peer = partner(axis, bit)
        n //= 2
        give = at(off + (1 - one) * n, n)
        off = off + one * n
        buf = recv[len(result)]
        reducing(send(live.at[give, lane], buf, peer), at(off, n), live, buf)
        live = acc
        path.append((off, n, peer))
    for axis, bit in whole:
        _, peer = partner(axis, bit)
        buf = recv[len(result)]
        where = at(off, n)
        reducing(send(acc.at[where, lane], buf, peer), where, acc, buf)
    for index, (off, n, peer) in enumerate(path[::-1]):
        where = at(off, n)
        copy = send(out.at[where, lane], out.at[where, lane], peer)

        def start(copy=copy, where=where, first=index == 0):
            if first:
                out[where, lane] = acc[where, lane]
            copy.start()

        result.append((start, copy.wait))
    return result


def orders(col_bits):
    return [col_bits, col_bits[:1] + col_bits[1:][::-1]]


def recv_shapes(rows, width, halving, whole):
    shapes = []
    for _ in range(halving):
        rows //= 2
        shapes.append(pltpu.VMEM((rows, width), F32))
    return shapes + [pltpu.VMEM((rows, width), F32)] * whole


def row_of(x, k):
    return jnp.broadcast_to(x[k:k + 1, :], x.shape)


def factor_block(d, m, tick):
    size = d.shape[0]
    tall = size // TICKS
    tiles = tall // 8
    sub = lax.broadcasted_iota(jnp.int32, (8, size), 0)
    done = []
    for hb in range(TICKS):
        tick(hb)
        panel = [d[8 * t:8 * t + 8] for t in range(tiles)]
        right = [m[8 * t:8 * t + 8] for t in range(tiles)]
        for g in range(tiles):
            base = hb * tall + 8 * g
            cols = {
                (t, j): jnp.broadcast_to(panel[t][:, base + j:base + j + 1], (8, size))
                for t in range(g, tiles) for j in range(8)
            }
            for k in range(8):
                lead = cols[g, k]
                inv = lax.rsqrt(row_of(lead, k))
                inv2 = inv * inv
                up, um = row_of(panel[g], k) * inv, row_of(right[g], k) * inv
                ahead = {j: row_of(lead, j) for j in range(k + 1, 8)}
                for t in range(g, tiles):
                    scaled = cols[t, k] * inv2
                    for j in range(k + 1, 8):
                        cols[t, j] = cols[t, j] - scaled * ahead[j]
                    low = cols[t, k] * inv
                    if t == g:
                        low = jnp.where(sub > k, low, 0.0)
                    panel[t] = panel[t] - low * up
                    right[t] = right[t] - low * um
                panel[g] = jnp.where(sub == k, up, panel[g])
                right[g] = jnp.where(sub == k, um, right[g])
        panel, right = jnp.concatenate(panel, axis=0), jnp.concatenate(right, axis=0)
        done.append(right)
        if hb + 1 < TICKS:
            both = jnp.concatenate([panel, right], axis=1)
            step = lax.dot_general(panel, both, (((0,), (0,)), ((), ())), precision=HI, preferred_element_type=F32)
            step = step[tall * (hb + 1):]
            d = d[tall:] - step[:, :size]
            m = m[tall:] - step[:, size:]
    return jnp.concatenate(done, axis=0)


NB = 128
TICKS = 4


def update_kernel(col_bits, row_bits, prior_ref, obs_ref, noise_ref, inv_ref, a_ref, b_ref, s_part, a_part, b_part, one_ref,
                  s_ref, sm, *rest):
    send_sem, recv_sem = rest[-2:]
    pick_rows(prior_ref, obs_ref, one_ref, s_part, b_part)
    (s_acc, a_acc, b_acc), bufs = rest[:3], list(rest[3:-2])
    obs = s_part.shape[0]
    col_axes = [[("col", b) for b in order] for order in orders(col_bits)]
    row_axes = [("row", b) for b in row_bits]
    greet(col_axes[0] + row_axes)
    sems = [0]

    def plan(src, out, acc, lanes, halving, whole):
        count = len(halving) + len(whole)
        mine = [bufs.pop(0) for _ in range(count)]
        steps = phases(src, out, acc, mine, send_sem, recv_sem, sems[0], lanes, halving, whole)
        sems[0] += len(steps)
        return steps

    width = obs // 2
    s_plans = [plan(s_part, s_ref, s_acc, (i * width, width), col_axes[i], row_axes) for i in range(2)]
    a_plans = [plan(a_part, a_ref, a_acc, (i * width, width), col_axes[i], []) for i in range(2)]
    b_plan = plan(b_part, b_ref, b_acc, (0, b_part.shape[1]), row_axes, [])

    for step in range(len(s_plans[0])):
        for steps in s_plans:
            steps[step][0]()
        if step == len(col_bits) + len(row_bits):
            b_plan[0][0]()
        if step < 2:
            half = prior_ref.shape[0] // TILE // 2
            pick_columns(prior_ref, one_ref, a_part, step * half, (step + 1) * half)
        for steps in s_plans:
            steps[step][1]()

    total = TICKS * (obs // NB)
    actions = [[] for _ in range(total + 1)]
    for steps, span, begun in [(a_plans[0], total, False), (a_plans[1], total, False), (b_plan, total - 1, True)]:
        if not begun:
            actions[0].append(steps[0][0])
        for index in range(len(steps)):
            slot = actions[round(span * (index + 1) / len(steps))]
            slot.append(steps[index][1])
            if index + 1 < len(steps):
                slot.append(steps[index + 1][0])

    i = lax.broadcasted_iota(jnp.int32, (obs, obs), 0)
    j = lax.broadcasted_iota(jnp.int32, (obs, obs), 1)
    sm[:, :obs] = s_ref[...] + jnp.where(i == j, noise_ref[...], 0.0)
    sm[:, obs:] = jnp.where(i == j, 1.0, 0.0)
    eye = jnp.where(i[:NB, :NB] == j[:NB, :NB], 1.0, 0.0).astype(F32)
    wide = lax.broadcasted_iota(jnp.int32, (NB, obs), 1)

    @pl.loop(0, obs // NB)
    def _(kb):
        def tick(mb):
            for block in range(obs // NB):
                todo = actions[block * TICKS + mb]
                if todo:
                    @pl.when(kb == block)
                    def _():
                        for act in todo:
                            act()

        at = pl.ds(pl.multiple_of(kb * NB, NB), NB)
        linv = factor_block(sm[at, at], eye, tick)
        row = jnp.dot(linv, sm[at, :], precision=HI, preferred_element_type=F32)
        inv_ref[at, :] = row[:, obs:]
        below = jnp.where(wide >= (kb + 1) * NB, row[:, :obs], 0.0)
        sm[...] -= lax.dot_general(below, row, (((0,), (0,)), ((), ())), precision=HI, preferred_element_type=F32)

    for act in actions[total]:
        act()


def update_parts(prior, observed, noise, mesh):
    (rows, cols), obs = prior.shape, observed.shape[0]
    col_bits, row_bits = bits(mesh.shape["col"]), bits(mesh.shape["row"])
    nc, nr = len(col_bits), len(row_bits)
    copies = 2 * (2 * nc + nr) + 2 * 2 * nc + 2 * nr
    like = jax.ShapeDtypeStruct
    return pl.pallas_call(
        functools.partial(update_kernel, col_bits, row_bits),
        name="update_parts",
        out_shape=(like((obs, obs), F32), like((rows, obs), F32), like((obs, cols), F32)),
        in_specs=[VMEM] * 3,
        out_specs=(VMEM,) * 3,
        scratch_shapes=[
            pltpu.VMEM((obs, obs), F32),
            pltpu.VMEM((rows, obs), F32),
            pltpu.VMEM((obs, cols), F32),
            pltpu.VMEM((cols, obs), BF16),
            pltpu.VMEM((obs, obs), F32),
            pltpu.VMEM((obs, 2 * obs), F32),
            pltpu.VMEM((obs, obs), F32),
            pltpu.VMEM((rows, obs), F32),
            pltpu.VMEM((obs, cols), F32),
        ]
        + recv_shapes(obs, obs // 2, nc, nr) * 2
        + recv_shapes(rows, obs // 2, nc, 0) * 2
        + recv_shapes(obs, cols, nr, 0)
        + [pltpu.SemaphoreType.DMA((copies,)), pltpu.SemaphoreType.DMA((copies,))],
        compiler_params=pltpu.CompilerParams(collective_id=0, has_side_effects=True, vmem_limit_bytes=LIMIT),
    )(prior, observed[None, :], noise[None, :])


def local(mesh, prior, observed, obs_noise):
    linv, a, b = update_parts(prior, observed, obs_noise, mesh)
    v = jnp.dot(linv, b, precision=MID, preferred_element_type=F32)
    y = jnp.dot(linv.T, v, precision=MID, preferred_element_type=F32)
    return prior - jnp.dot(a, y, precision=MID, preferred_element_type=F32)


def solution(mesh):
    return jax.shard_map(
        functools.partial(local, mesh),
        mesh=mesh,
        in_specs=(P("row", "col"), P(), P()),
        out_specs=P("row", "col"),
        check_vma=False,
    )
```

```python
import functools

import jax
import jax.numpy as jnp
from jax import lax
from jax.experimental import pallas as pl
from jax.experimental.pallas import tpu as pltpu
from jax.sharding import PartitionSpec as P

F32 = jnp.float32
BF16 = jnp.bfloat16
HI = lax.Precision.HIGHEST
MID = lax.Precision.HIGH
MESH = pl.DeviceIdType.MESH
VMEM = pl.BlockSpec(memory_space=pltpu.VMEM)
LIMIT = 60 * 1024 * 1024


def parts3(x):
    first = x.astype(BF16)
    rest = x - first.astype(F32)
    second = rest.astype(BF16)
    third = (rest - second.astype(F32)).astype(BF16)
    return first, second, third


def dot(a, b):
    return jnp.dot(a, b, preferred_element_type=F32)


TILE = 256


def pick_rows(prior_ref, obs_ref, one_ref, s_ref, b_ref):
    rows, cols = prior_ref.shape
    obs = obs_ref.shape[1]
    row_start = lax.axis_index("row") * rows
    col_start = lax.axis_index("col") * cols
    in_cols = lax.broadcasted_iota(jnp.int32, (cols, obs), 0) == obs_ref[...] - col_start
    one_ref[...] = jnp.where(in_cols, 1.0, 0.0).astype(BF16)
    tall = jnp.broadcast_to(obs_ref[...].astype(F32), (8, obs)).T[:, :1].astype(jnp.int32)

    @pl.loop(0, rows // TILE)
    def _(t):
        at = pl.ds(pl.multiple_of(t * TILE, TILE), TILE)
        p1, p2, p3 = parts3(prior_ref[at, :])
        left = lax.broadcasted_iota(jnp.int32, (obs, TILE), 1) == tall - (row_start + t * TILE)
        left = jnp.where(left, 1.0, 0.0).astype(BF16)
        got = dot(left, p1) + dot(left, p2) + dot(left, p3)

        @pl.when(t == 0)
        def _():
            b_ref[...] = got

        @pl.when(t > 0)
        def _():
            b_ref[...] += got

    @pl.loop(0, obs // TILE)
    def _(t):
        at = pl.ds(pl.multiple_of(t * TILE, TILE), TILE)
        g1, g2, g3 = parts3(b_ref[at, :])
        pick = one_ref[...]
        s_ref[at, :] = dot(g1, pick) + dot(g2, pick) + dot(g3, pick)


def pick_columns(prior_ref, one_ref, a_ref, first, last):
    @pl.loop(first, last)
    def _(t):
        at = pl.ds(pl.multiple_of(t * TILE, TILE), TILE)
        p1, p2, p3 = parts3(prior_ref[at, :])
        pick = one_ref[...]
        a_ref[at, :] = dot(p1, pick) + dot(p2, pick) + dot(p3, pick)


def bits(size):
    return list(range(size.bit_length() - 1))


def partner(axis, bit):
    me = lax.axis_index(axis)
    one = (me // (1 << bit)) % 2
    return one, {axis: me + (1 - 2 * one) * (1 << bit)}


def greet(axes):
    barrier = pltpu.get_barrier_semaphore()
    for axis, bit in axes:
        _, peer = partner(axis, bit)
        pl.semaphore_signal(barrier, inc=1, device_id=peer, device_id_type=MESH)
    pl.semaphore_wait(barrier, len(axes))


def phases(src, out, acc, recv, send_sem, recv_sem, first_sem, lanes, halving, whole):
    lane = pl.ds(lanes[0], lanes[1])
    off, n, live = 0, src.shape[0], src
    result, path = [], []

    def at(off, n):
        return pl.ds(pl.multiple_of(off, 8), n)

    def send(source, target, peer):
        sem = first_sem + len(result)
        return pltpu.make_async_remote_copy(
            source, target, send_sem.at[sem], recv_sem.at[sem], device_id=peer, device_id_type=MESH)

    def reducing(copy, where, live, buf):
        def finish():
            copy.wait()
            acc[where, lane] = live[where, lane] + buf[...]

        result.append((copy.start, finish))

    for axis, bit in halving:
        one, peer = partner(axis, bit)
        n //= 2
        give = at(off + (1 - one) * n, n)
        off = off + one * n
        buf = recv[len(result)]
        reducing(send(live.at[give, lane], buf, peer), at(off, n), live, buf)
        live = acc
        path.append((off, n, peer))
    for axis, bit in whole:
        _, peer = partner(axis, bit)
        buf = recv[len(result)]
        where = at(off, n)
        reducing(send(acc.at[where, lane], buf, peer), where, acc, buf)
    for index, (off, n, peer) in enumerate(path[::-1]):
        where = at(off, n)
        copy = send(out.at[where, lane], out.at[where, lane], peer)

        def start(copy=copy, where=where, first=index == 0):
            if first:
                out[where, lane] = acc[where, lane]
            copy.start()

        result.append((start, copy.wait))
    return result


def orders(col_bits):
    return [col_bits, col_bits[:1] + col_bits[1:][::-1]]


def recv_shapes(rows, width, halving, whole):
    shapes = []
    for _ in range(halving):
        rows //= 2
        shapes.append(pltpu.VMEM((rows, width), F32))
    return shapes + [pltpu.VMEM((rows, width), F32)] * whole


def row_of(x, k):
    return jnp.broadcast_to(x[k:k + 1, :], x.shape)


def factor_block(d, m, tick):
    size = d.shape[0]
    tall = size // TICKS
    tiles = tall // 8
    sub = lax.broadcasted_iota(jnp.int32, (8, size), 0)
    done = []
    for hb in range(TICKS):
        tick(hb)
        panel = [d[8 * t:8 * t + 8] for t in range(tiles)]
        right = [m[8 * t:8 * t + 8] for t in range(tiles)]
        for g in range(tiles):
            base = hb * tall + 8 * g
            cols = {
                (t, j): jnp.broadcast_to(panel[t][:, base + j:base + j + 1], (8, size))
                for t in range(g, tiles) for j in range(8)
            }
            for k in range(8):
                lead = cols[g, k]
                inv = lax.rsqrt(row_of(lead, k))
                inv2 = inv * inv
                up, um = row_of(panel[g], k) * inv, row_of(right[g], k) * inv
                ahead = {j: row_of(lead, j) for j in range(k + 1, 8)}
                for t in range(g, tiles):
                    scaled = cols[t, k] * inv2
                    for j in range(k + 1, 8):
                        cols[t, j] = cols[t, j] - scaled * ahead[j]
                    low = cols[t, k] * inv
                    if t == g:
                        low = jnp.where(sub > k, low, 0.0)
                    panel[t] = panel[t] - low * up
                    right[t] = right[t] - low * um
                panel[g] = jnp.where(sub == k, up, panel[g])
                right[g] = jnp.where(sub == k, um, right[g])
        panel, right = jnp.concatenate(panel, axis=0), jnp.concatenate(right, axis=0)
        done.append(right)
        if hb + 1 < TICKS:
            both = jnp.concatenate([panel, right], axis=1)
            step = lax.dot_general(panel, both, (((0,), (0,)), ((), ())), precision=HI, preferred_element_type=F32)
            step = step[tall * (hb + 1):]
            d = d[tall:] - step[:, :size]
            m = m[tall:] - step[:, size:]
    return jnp.concatenate(done, axis=0)


NB = 128
TICKS = 4


def update_kernel(col_bits, row_bits, prior_ref, obs_ref, noise_ref, inv_ref, a_ref, b_ref, s_part, a_part, b_part, one_ref,
                  s_ref, sm, *rest):
    send_sem, recv_sem = rest[-2:]
    pick_rows(prior_ref, obs_ref, one_ref, s_part, b_part)
    (s_acc, a_acc, b_acc), bufs = rest[:3], list(rest[3:-2])
    obs = s_part.shape[0]
    col_axes = [[("col", b) for b in order] for order in orders(col_bits)]
    row_axes = [("row", b) for b in row_bits]
    greet(col_axes[0] + row_axes)
    sems = [0]

    def plan(src, out, acc, lanes, halving, whole):
        count = len(halving) + len(whole)
        mine = [bufs.pop(0) for _ in range(count)]
        steps = phases(src, out, acc, mine, send_sem, recv_sem, sems[0], lanes, halving, whole)
        sems[0] += len(steps)
        return steps

    width = obs // 2
    s_plans = [plan(s_part, s_ref, s_acc, (i * width, width), col_axes[i], row_axes) for i in range(2)]
    a_plans = [plan(a_part, a_ref, a_acc, (i * width, width), col_axes[i], []) for i in range(2)]
    b_plan = plan(b_part, b_ref, b_acc, (0, b_part.shape[1]), row_axes, [])

    nc, nr = len(col_bits), len(row_bits)
    early = min(2, nr)
    for step in range(len(s_plans[0])):
        for steps in s_plans:
            steps[step][0]()
        if step == 0:
            b_plan[0][0]()
        if step < 2:
            half = prior_ref.shape[0] // TILE // 2
            pick_columns(prior_ref, one_ref, a_part, step * half, (step + 1) * half)
        if nc <= step < nc + early:
            for steps in a_plans:
                steps[step - nc][0]()
        if step == nc + nr:
            b_plan[1][0]()
        for steps in s_plans:
            steps[step][1]()
        if step == nc - 1:
            b_plan[0][1]()
        if nc <= step < nc + early:
            for steps in a_plans:
                steps[step - nc][1]()

    total = TICKS * (obs // NB)
    actions = [[] for _ in range(total + 1)]
    for steps in a_plans:
        left = steps[early:]
        actions[0].append(left[0][0])
        for index in range(len(left)):
            slot = actions[round((total - 1) * (index + 1) / len(left))]
            slot.append(left[index][1])
            slot += [step[0] for step in left[index + 1:index + 2]]
    left = b_plan[1:]
    for index in range(len(left)):
        slot = actions[1 + round((total - 1) * index / (len(left) - 1))]
        slot.append(left[index][1])
        slot += [step[0] for step in left[index + 1:index + 2]]

    i = lax.broadcasted_iota(jnp.int32, (obs, obs), 0)
    j = lax.broadcasted_iota(jnp.int32, (obs, obs), 1)
    sm[:, :obs] = s_ref[...] + jnp.where(i == j, noise_ref[...], 0.0)
    sm[:, obs:] = jnp.where(i == j, 1.0, 0.0)
    eye = jnp.where(i[:NB, :NB] == j[:NB, :NB], 1.0, 0.0).astype(F32)
    wide = lax.broadcasted_iota(jnp.int32, (NB, obs), 1)

    @pl.loop(0, obs // NB)
    def _(kb):
        def tick(mb):
            for block in range(obs // NB):
                todo = actions[block * TICKS + mb]
                if todo:
                    @pl.when(kb == block)
                    def _():
                        for act in todo:
                            act()

        at = pl.ds(pl.multiple_of(kb * NB, NB), NB)
        linv = factor_block(sm[at, at], eye, tick)
        row = jnp.dot(linv, sm[at, :], precision=HI, preferred_element_type=F32)
        inv_ref[at, :] = row[:, obs:]
        below = jnp.where(wide >= (kb + 1) * NB, row[:, :obs], 0.0)
        sm[...] -= lax.dot_general(below, row, (((0,), (0,)), ((), ())), precision=HI, preferred_element_type=F32)

    for act in actions[total]:
        act()


def update_parts(prior, observed, noise, mesh):
    (rows, cols), obs = prior.shape, observed.shape[0]
    col_bits, row_bits = bits(mesh.shape["col"]), bits(mesh.shape["row"])
    nc, nr = len(col_bits), len(row_bits)
    copies = 2 * (2 * nc + nr) + 2 * 2 * nc + 2 * nr
    like = jax.ShapeDtypeStruct
    return pl.pallas_call(
        functools.partial(update_kernel, col_bits, row_bits),
        name="update_parts",
        out_shape=(like((obs, obs), F32), like((rows, obs), F32), like((obs, cols), F32)),
        in_specs=[VMEM] * 3,
        out_specs=(VMEM,) * 3,
        scratch_shapes=[
            pltpu.VMEM((obs, obs), F32),
            pltpu.VMEM((rows, obs), F32),
            pltpu.VMEM((obs, cols), F32),
            pltpu.VMEM((cols, obs), BF16),
            pltpu.VMEM((obs, obs), F32),
            pltpu.VMEM((obs, 2 * obs), F32),
            pltpu.VMEM((obs, obs), F32),
            pltpu.VMEM((rows, obs), F32),
            pltpu.VMEM((obs, cols), F32),
        ]
        + recv_shapes(obs, obs // 2, nc, nr) * 2
        + recv_shapes(rows, obs // 2, nc, 0) * 2
        + recv_shapes(obs, cols, nr, 0)
        + [pltpu.SemaphoreType.DMA((copies,)), pltpu.SemaphoreType.DMA((copies,))],
        compiler_params=pltpu.CompilerParams(collective_id=0, has_side_effects=True, vmem_limit_bytes=LIMIT),
    )(prior, observed[None, :], noise[None, :])


def local(mesh, prior, observed, obs_noise):
    linv, a, b = update_parts(prior, observed, obs_noise, mesh)
    v = jnp.dot(linv, b, precision=MID, preferred_element_type=F32)
    y = jnp.dot(linv.T, v, precision=MID, preferred_element_type=F32)
    return prior - jnp.dot(a, y, precision=MID, preferred_element_type=F32)


def solution(mesh):
    return jax.shard_map(
        functools.partial(local, mesh),
        mesh=mesh,
        in_specs=(P("row", "col"), P(), P()),
        out_specs=P("row", "col"),
        check_vma=False,
    )
```

```python
import functools

import jax
import jax.numpy as jnp
from jax import lax
from jax.experimental import pallas as pl
from jax.experimental.pallas import tpu as pltpu
from jax.sharding import PartitionSpec as P

F32 = jnp.float32
BF16 = jnp.bfloat16
HI = lax.Precision.HIGHEST
MID = lax.Precision.HIGH
MESH = pl.DeviceIdType.MESH
VMEM = pl.BlockSpec(memory_space=pltpu.VMEM)
LIMIT = 60 * 1024 * 1024


def parts3(x):
    first = x.astype(BF16)
    rest = x - first.astype(F32)
    second = rest.astype(BF16)
    third = (rest - second.astype(F32)).astype(BF16)
    return first, second, third


def dot(a, b):
    return jnp.dot(a, b, preferred_element_type=F32)


TILE = 256


def pick_rows(prior_ref, obs_ref, one_ref, s_ref, b_ref):
    rows, cols = prior_ref.shape
    obs = obs_ref.shape[1]
    row_start = lax.axis_index("row") * rows
    col_start = lax.axis_index("col") * cols
    in_cols = lax.broadcasted_iota(jnp.int32, (cols, obs), 0) == obs_ref[...] - col_start
    one_ref[...] = jnp.where(in_cols, 1.0, 0.0).astype(BF16)
    tall = jnp.broadcast_to(obs_ref[...].astype(F32), (8, obs)).T[:, :1].astype(jnp.int32)

    @pl.loop(0, rows // TILE)
    def _(t):
        at = pl.ds(pl.multiple_of(t * TILE, TILE), TILE)
        p1, p2, p3 = parts3(prior_ref[at, :])
        left = lax.broadcasted_iota(jnp.int32, (obs, TILE), 1) == tall - (row_start + t * TILE)
        left = jnp.where(left, 1.0, 0.0).astype(BF16)
        got = dot(left, p1) + dot(left, p2) + dot(left, p3)

        @pl.when(t == 0)
        def _():
            b_ref[...] = got

        @pl.when(t > 0)
        def _():
            b_ref[...] += got

    @pl.loop(0, obs // TILE)
    def _(t):
        at = pl.ds(pl.multiple_of(t * TILE, TILE), TILE)
        g1, g2, g3 = parts3(b_ref[at, :])
        pick = one_ref[...]
        s_ref[at, :obs] = dot(g1, pick) + dot(g2, pick) + dot(g3, pick)


def packed_blocks(obs):
    q = obs // 4
    h = q // 2
    return [
        ((0, q, 0, obs), (0, 0)),
        ((q, q, q, obs - q), (q, q)),
        ((q, q, 0, q), (3 * q, 3 * q)),
        ((2 * q, h, 0, 2 * q), (2 * q, 2 * q)),
        ((2 * q, h, 2 * q, 2 * q), (2 * q + h, 2 * q)),
    ]


def halvings(rows, col_bits):
    count = 0
    while count < len(col_bits) and (rows >> (count + 1)) % 8 == 0:
        count += 1
    return count


def pick_columns(prior_ref, one_ref, a_ref, first, last):
    @pl.loop(first, last)
    def _(t):
        at = pl.ds(pl.multiple_of(t * TILE, TILE), TILE)
        p1, p2, p3 = parts3(prior_ref[at, :])
        pick = one_ref[...]
        a_ref[at, :] = dot(p1, pick) + dot(p2, pick) + dot(p3, pick)


def bits(size):
    return list(range(size.bit_length() - 1))


def partner(axis, bit):
    me = lax.axis_index(axis)
    one = (me // (1 << bit)) % 2
    return one, {axis: me + (1 - 2 * one) * (1 << bit)}


def greet(axes):
    barrier = pltpu.get_barrier_semaphore()
    for axis, bit in axes:
        _, peer = partner(axis, bit)
        pl.semaphore_signal(barrier, inc=1, device_id=peer, device_id_type=MESH)
    pl.semaphore_wait(barrier, len(axes))


def phases(src, out, acc, recv, send_sem, recv_sem, first_sem, lanes, halving, whole):
    lane = pl.ds(lanes[0], lanes[1])
    off, n, live = 0, src.shape[0], src
    result, path = [], []

    def at(off, n):
        return pl.ds(pl.multiple_of(off, 8), n)

    def send(source, target, peer):
        sem = first_sem + len(result)
        return pltpu.make_async_remote_copy(
            source, target, send_sem.at[sem], recv_sem.at[sem], device_id=peer, device_id_type=MESH)

    def reducing(copy, where, live, buf):
        def finish():
            copy.wait()
            acc[where, lane] = live[where, lane] + buf[...]

        result.append((copy.start, finish))

    for axis, bit in halving:
        one, peer = partner(axis, bit)
        n //= 2
        give = at(off + (1 - one) * n, n)
        off = off + one * n
        buf = recv[len(result)]
        reducing(send(live.at[give, lane], buf, peer), at(off, n), live, buf)
        live = acc
        path.append((off, n, peer))
    for axis, bit in whole:
        _, peer = partner(axis, bit)
        buf = recv[len(result)]
        where = at(off, n)
        reducing(send(acc.at[where, lane], buf, peer), where, acc, buf)
    for index, (off, n, peer) in enumerate(path[::-1]):
        where = at(off, n)
        copy = send(out.at[where, lane], out.at[where, lane], peer)

        def start(copy=copy, where=where, first=index == 0):
            if first:
                out[where, lane] = acc[where, lane]
            copy.start()

        result.append((start, copy.wait))
    return result


def orders(col_bits):
    return [col_bits, col_bits[:1] + col_bits[1:][::-1]]


def recv_shapes(rows, width, halving, whole):
    shapes = []
    for _ in range(halving):
        rows //= 2
        shapes.append(pltpu.VMEM((rows, width), F32))
    return shapes + [pltpu.VMEM((rows, width), F32)] * whole


def row_of(x, k):
    return jnp.broadcast_to(x[k:k + 1, :], x.shape)


def factor_block(d, m, tick):
    size = d.shape[0]
    tall = size // TICKS
    tiles = tall // 8
    sub = lax.broadcasted_iota(jnp.int32, (8, size), 0)
    done = []
    for hb in range(TICKS):
        tick(hb)
        panel = [d[8 * t:8 * t + 8] for t in range(tiles)]
        right = [m[8 * t:8 * t + 8] for t in range(tiles)]
        for g in range(tiles):
            base = hb * tall + 8 * g
            cols = {
                (t, j): jnp.broadcast_to(panel[t][:, base + j:base + j + 1], (8, size))
                for t in range(g, tiles) for j in range(8)
            }
            for k in range(8):
                lead = cols[g, k]
                inv = lax.rsqrt(row_of(lead, k))
                inv2 = inv * inv
                up, um = row_of(panel[g], k) * inv, row_of(right[g], k) * inv
                ahead = {j: row_of(lead, j) for j in range(k + 1, 8)}
                for t in range(g, tiles):
                    scaled = cols[t, k] * inv2
                    for j in range(k + 1, 8):
                        cols[t, j] = cols[t, j] - scaled * ahead[j]
                    low = cols[t, k] * inv
                    if t == g:
                        low = jnp.where(sub > k, low, 0.0)
                    panel[t] = panel[t] - low * up
                    right[t] = right[t] - low * um
                panel[g] = jnp.where(sub == k, up, panel[g])
                right[g] = jnp.where(sub == k, um, right[g])
        panel, right = jnp.concatenate(panel, axis=0), jnp.concatenate(right, axis=0)
        done.append(right)
        if hb + 1 < TICKS:
            both = jnp.concatenate([panel, right], axis=1)
            step = lax.dot_general(panel, both, (((0,), (0,)), ((), ())), precision=HI, preferred_element_type=F32)
            step = step[tall * (hb + 1):]
            d = d[tall:] - step[:, :size]
            m = m[tall:] - step[:, size:]
    return jnp.concatenate(done, axis=0)


NB = 128
TICKS = 4


def update_kernel(col_bits, row_bits, prior_ref, obs_ref, noise_ref, inv_ref, a_ref, b_ref, s_part, a_part, b_part, one_ref,
                  s_ref, sm, *rest):
    send_sem, recv_sem = rest[-2:]
    obs = obs_ref.shape[1]
    pick_rows(prior_ref, obs_ref, one_ref, sm, b_part)
    for (r, n, c, w), (y, x) in packed_blocks(obs):
        s_part[r:r + n, c:c + w] = sm[y:y + n, x:x + w]
    (s_acc, a_acc, b_acc), bufs = rest[:3], list(rest[3:-2])
    col_axes = [[("col", b) for b in order] for order in orders(col_bits)]
    row_axes = [("row", b) for b in row_bits]
    greet(col_axes[0] + row_axes)
    sems = [0]

    def plan(src, out, acc, lanes, halving, whole):
        count = len(halving) + len(whole)
        mine = [bufs.pop(0) for _ in range(count)]
        steps = phases(src, out, acc, mine, send_sem, recv_sem, sems[0], lanes, halving, whole)
        sems[0] += len(steps)
        return steps

    width = obs // 2
    cut = halvings(s_part.shape[0], col_bits)
    s_plans = [
        plan(s_part, s_ref, s_acc, (i * width, width), col_axes[i][:cut], col_axes[i][cut:] + row_axes) for i in range(2)
    ]
    a_plans = [plan(a_part, a_ref, a_acc, (i * width, width), col_axes[i], []) for i in range(2)]
    wide = b_part.shape[1] // 2
    b_plans = [plan(b_part, b_ref, b_acc, (i * wide, wide), row_axes, []) for i in range(2)]

    nc, nr = len(col_bits), len(row_bits)
    early = min(2, nr)
    for step in range(len(s_plans[0])):
        for steps in s_plans:
            steps[step][0]()
        if step == 0:
            for steps in b_plans:
                steps[0][0]()
        if step < 2:
            half = prior_ref.shape[0] // TILE // 2
            pick_columns(prior_ref, one_ref, a_part, step * half, (step + 1) * half)
        if nc <= step < nc + early:
            for steps in a_plans:
                steps[step - nc][0]()
        if step == nc + nr:
            for steps in b_plans:
                steps[1][0]()
        for steps in s_plans:
            steps[step][1]()
        if step == nc - 1:
            for steps in b_plans:
                steps[0][1]()
        if nc <= step < nc + early:
            for steps in a_plans:
                steps[step - nc][1]()

    total = TICKS * (obs // NB)
    actions = [[] for _ in range(total + 1)]
    for steps in a_plans:
        left = steps[early:]
        actions[0].append(left[0][0])
        for index in range(len(left)):
            slot = actions[round((total - 1) * (index + 1) / len(left))]
            slot.append(left[index][1])
            slot += [step[0] for step in left[index + 1:index + 2]]
    for stream, steps in enumerate(b_plans):
        left = steps[1:]
        for index in range(len(left)):
            slot = actions[round(total * (2 * index + stream) / (2 * len(left) - 1))]
            slot.append(left[index][1])
            slot += [step[0] for step in left[index + 1:index + 2]]

    i = lax.broadcasted_iota(jnp.int32, (obs, obs), 0)
    j = lax.broadcasted_iota(jnp.int32, (obs, obs), 1)
    sm[:, :obs] = jnp.zeros((obs, obs), F32)
    for (r, n, c, w), (y, x) in packed_blocks(obs):
        sm[y:y + n, x:x + w] = s_ref[r:r + n, c:c + w]
    sm[:, :obs] += jnp.where(i == j, noise_ref[...], 0.0)
    sm[:, obs:] = jnp.where(i == j, 1.0, 0.0)
    eye = jnp.where(i[:NB, :NB] == j[:NB, :NB], 1.0, 0.0).astype(F32)
    wide = lax.broadcasted_iota(jnp.int32, (NB, obs), 1)

    @pl.loop(0, obs // NB)
    def _(kb):
        def tick(mb):
            for block in range(obs // NB):
                todo = actions[block * TICKS + mb]
                if todo:
                    @pl.when(kb == block)
                    def _():
                        for act in todo:
                            act()

        at = pl.ds(pl.multiple_of(kb * NB, NB), NB)
        linv = factor_block(sm[at, at], eye, tick)
        row = jnp.dot(linv, sm[at, :], precision=HI, preferred_element_type=F32)
        inv_ref[at, :] = row[:, obs:]
        below = jnp.where(wide >= (kb + 1) * NB, row[:, :obs], 0.0)
        sm[...] -= lax.dot_general(below, row, (((0,), (0,)), ((), ())), precision=HI, preferred_element_type=F32)

    for act in actions[total]:
        act()


def update_parts(prior, observed, noise, mesh):
    (rows, cols), obs = prior.shape, observed.shape[0]
    col_bits, row_bits = bits(mesh.shape["col"]), bits(mesh.shape["row"])
    nc, nr = len(col_bits), len(row_bits)
    packed = 5 * obs // 8
    cut = halvings(packed, col_bits)
    copies = 2 * (nc + cut + nr) + 2 * 2 * nc + 2 * 2 * nr
    like = jax.ShapeDtypeStruct
    return pl.pallas_call(
        functools.partial(update_kernel, col_bits, row_bits),
        name="update_parts",
        out_shape=(like((obs, obs), F32), like((rows, obs), F32), like((obs, cols), F32)),
        in_specs=[VMEM] * 3,
        out_specs=(VMEM,) * 3,
        scratch_shapes=[
            pltpu.VMEM((packed, obs), F32),
            pltpu.VMEM((rows, obs), F32),
            pltpu.VMEM((obs, cols), F32),
            pltpu.VMEM((cols, obs), BF16),
            pltpu.VMEM((packed, obs), F32),
            pltpu.VMEM((obs, 2 * obs), F32),
            pltpu.VMEM((packed, obs), F32),
            pltpu.VMEM((rows, obs), F32),
            pltpu.VMEM((obs, cols), F32),
        ]
        + recv_shapes(packed, obs // 2, cut, nc - cut + nr) * 2
        + recv_shapes(rows, obs // 2, nc, 0) * 2
        + recv_shapes(obs, cols // 2, nr, 0) * 2
        + [pltpu.SemaphoreType.DMA((copies,)), pltpu.SemaphoreType.DMA((copies,))],
        compiler_params=pltpu.CompilerParams(collective_id=0, has_side_effects=True, vmem_limit_bytes=LIMIT),
    )(prior, observed[None, :], noise[None, :])


def local(mesh, prior, observed, obs_noise):
    linv, a, b = update_parts(prior, observed, obs_noise, mesh)
    v = jnp.dot(linv, b, precision=MID, preferred_element_type=F32)
    y = jnp.dot(linv.T, v, precision=MID, preferred_element_type=F32)
    return prior - jnp.dot(a, y, precision=MID, preferred_element_type=F32)


def solution(mesh):
    return jax.shard_map(
        functools.partial(local, mesh),
        mesh=mesh,
        in_specs=(P("row", "col"), P(), P()),
        out_specs=P("row", "col"),
        check_vma=False,
    )
```

```python
import functools

import jax
import jax.numpy as jnp
from jax import lax
from jax.experimental import pallas as pl
from jax.experimental.pallas import tpu as pltpu
from jax.sharding import PartitionSpec as P

F32 = jnp.float32
BF16 = jnp.bfloat16
HI = lax.Precision.HIGHEST
MID = lax.Precision.HIGH
MESH = pl.DeviceIdType.MESH
VMEM = pl.BlockSpec(memory_space=pltpu.VMEM)
LIMIT = 60 * 1024 * 1024


def parts3(x):
    first = x.astype(BF16)
    rest = x - first.astype(F32)
    second = rest.astype(BF16)
    third = (rest - second.astype(F32)).astype(BF16)
    return first, second, third


def dot(a, b):
    return jnp.dot(a, b, preferred_element_type=F32)


TILE = 256


def pick_rows(prior_ref, obs_ref, one_ref, s_ref, b_ref):
    rows, cols = prior_ref.shape
    obs = obs_ref.shape[1]
    row_start = lax.axis_index("row") * rows
    col_start = lax.axis_index("col") * cols
    in_cols = lax.broadcasted_iota(jnp.int32, (cols, obs), 0) == obs_ref[...] - col_start
    one_ref[...] = jnp.where(in_cols, 1.0, 0.0).astype(BF16)
    tall = jnp.broadcast_to(obs_ref[...].astype(F32), (8, obs)).T[:, :1].astype(jnp.int32)

    @pl.loop(0, rows // TILE)
    def _(t):
        at = pl.ds(pl.multiple_of(t * TILE, TILE), TILE)
        p1, p2, p3 = parts3(prior_ref[at, :])
        left = lax.broadcasted_iota(jnp.int32, (obs, TILE), 1) == tall - (row_start + t * TILE)
        left = jnp.where(left, 1.0, 0.0).astype(BF16)
        got = dot(left, p1) + dot(left, p2) + dot(left, p3)

        @pl.when(t == 0)
        def _():
            b_ref[...] = got

        @pl.when(t > 0)
        def _():
            b_ref[...] += got

    @pl.loop(0, obs // TILE)
    def _(t):
        at = pl.ds(pl.multiple_of(t * TILE, TILE), TILE)
        g1, g2, g3 = parts3(b_ref[at, :])
        pick = one_ref[...]
        s_ref[at, :obs] = dot(g1, pick) + dot(g2, pick) + dot(g3, pick)


def packed_blocks(obs):
    q = obs // 4
    h = q // 2
    return [
        ((0, q, 0, obs), (0, 0)),
        ((q, q, q, obs - q), (q, q)),
        ((q, q, 0, q), (3 * q, 3 * q)),
        ((2 * q, h, 0, 2 * q), (2 * q, 2 * q)),
        ((2 * q, h, 2 * q, 2 * q), (2 * q + h, 2 * q)),
    ]


def halvings(rows, col_bits):
    count = 0
    while count < len(col_bits) and (rows >> (count + 1)) % 8 == 0:
        count += 1
    return count


def pick_columns(prior_ref, one_ref, a_ref, first, last):
    @pl.loop(first, last)
    def _(t):
        at = pl.ds(pl.multiple_of(t * TILE, TILE), TILE)
        p1, p2, p3 = parts3(prior_ref[at, :])
        pick = one_ref[...]
        a_ref[at, :] = dot(p1, pick) + dot(p2, pick) + dot(p3, pick)


def bits(size):
    return list(range(size.bit_length() - 1))


def partner(axis, bit):
    me = lax.axis_index(axis)
    one = (me // (1 << bit)) % 2
    return one, {axis: me + (1 - 2 * one) * (1 << bit)}


def greet(axes):
    barrier = pltpu.get_barrier_semaphore()
    for axis, bit in axes:
        _, peer = partner(axis, bit)
        pl.semaphore_signal(barrier, inc=1, device_id=peer, device_id_type=MESH)
    pl.semaphore_wait(barrier, len(axes))


def phases(src, out, acc, recv, send_sem, recv_sem, first_sem, lanes, halving, whole):
    lane = pl.ds(lanes[0], lanes[1])
    off, n, live = 0, src.shape[0], src
    result, path = [], []

    def at(off, n):
        return pl.ds(pl.multiple_of(off, 8), n)

    def send(source, target, peer):
        sem = first_sem + len(result)
        return pltpu.make_async_remote_copy(
            source, target, send_sem.at[sem], recv_sem.at[sem], device_id=peer, device_id_type=MESH)

    def reducing(copy, where, live, buf):
        def finish():
            copy.wait()
            acc[where, lane] = live[where, lane] + buf[...]

        result.append((copy.start, finish))

    for axis, bit in halving:
        one, peer = partner(axis, bit)
        n //= 2
        give = at(off + (1 - one) * n, n)
        off = off + one * n
        buf = recv[len(result)]
        reducing(send(live.at[give, lane], buf, peer), at(off, n), live, buf)
        live = acc
        path.append((off, n, peer))
    for axis, bit in whole:
        _, peer = partner(axis, bit)
        buf = recv[len(result)]
        where = at(off, n)
        reducing(send(acc.at[where, lane], buf, peer), where, acc, buf)
    for index, (off, n, peer) in enumerate(path[::-1]):
        where = at(off, n)
        copy = send(out.at[where, lane], out.at[where, lane], peer)

        def start(copy=copy, where=where, first=index == 0):
            if first:
                out[where, lane] = acc[where, lane]
            copy.start()

        result.append((start, copy.wait))
    return result


def orders(col_bits):
    return [col_bits, col_bits[:1] + col_bits[1:][::-1]]


def recv_shapes(rows, width, halving, whole):
    shapes = []
    for _ in range(halving):
        rows //= 2
        shapes.append(pltpu.VMEM((rows, width), F32))
    return shapes + [pltpu.VMEM((rows, width), F32)] * whole


def row_of(x, k):
    return jnp.broadcast_to(x[k:k + 1, :], x.shape)


def factor_block(d, m, tick):
    size = d.shape[0]
    tall = size // TICKS
    tiles = tall // 8
    sub = lax.broadcasted_iota(jnp.int32, (8, size), 0)
    done = []
    for hb in range(TICKS):
        tick(hb)
        panel = [d[8 * t:8 * t + 8] for t in range(tiles)]
        right = [m[8 * t:8 * t + 8] for t in range(tiles)]
        for g in range(tiles):
            base = hb * tall + 8 * g
            cols = {
                (t, j): jnp.broadcast_to(panel[t][:, base + j:base + j + 1], (8, size))
                for t in range(g, tiles) for j in range(8)
            }
            for k in range(8):
                lead = cols[g, k]
                inv = lax.rsqrt(row_of(lead, k))
                inv2 = inv * inv
                up, um = row_of(panel[g], k) * inv, row_of(right[g], k) * inv
                ahead = {j: row_of(lead, j) for j in range(k + 1, 8)}
                for t in range(g, tiles):
                    scaled = cols[t, k] * inv2
                    for j in range(k + 1, 8):
                        cols[t, j] = cols[t, j] - scaled * ahead[j]
                    low = cols[t, k] * inv
                    if t == g:
                        low = jnp.where(sub > k, low, 0.0)
                    panel[t] = panel[t] - low * up
                    right[t] = right[t] - low * um
                panel[g] = jnp.where(sub == k, up, panel[g])
                right[g] = jnp.where(sub == k, um, right[g])
        panel, right = jnp.concatenate(panel, axis=0), jnp.concatenate(right, axis=0)
        done.append(right)
        if hb + 1 < TICKS:
            both = jnp.concatenate([panel, right], axis=1)
            step = lax.dot_general(panel, both, (((0,), (0,)), ((), ())), precision=HI, preferred_element_type=F32)
            step = step[tall * (hb + 1):]
            d = d[tall:] - step[:, :size]
            m = m[tall:] - step[:, size:]
    return jnp.concatenate(done, axis=0)


NB = 128
TICKS = 4


def update_kernel(col_bits, row_bits, prior_ref, obs_ref, noise_ref, inv_ref, a_ref, b_ref, s_part, a_part, b_part, one_ref,
                  s_ref, sm, *rest):
    send_sem, recv_sem = rest[-2:]
    obs = obs_ref.shape[1]
    pick_rows(prior_ref, obs_ref, one_ref, sm, b_part)
    for (r, n, c, w), (y, x) in packed_blocks(obs):
        s_part[r:r + n, c:c + w] = sm[y:y + n, x:x + w]
    (s_acc, a_acc, b_acc), bufs = rest[:3], list(rest[3:-2])
    col_axes = [[("col", b) for b in order] for order in orders(col_bits)]
    row_axes = [("row", b) for b in row_bits]
    greet(col_axes[0] + row_axes)
    sems = [0]

    def plan(src, out, acc, lanes, halving, whole):
        count = len(halving) + len(whole)
        mine = [bufs.pop(0) for _ in range(count)]
        steps = phases(src, out, acc, mine, send_sem, recv_sem, sems[0], lanes, halving, whole)
        sems[0] += len(steps)
        return steps

    width = obs // 2
    cut = halvings(s_part.shape[0], col_bits)
    s_plans = [
        plan(s_part, s_ref, s_acc, (i * width, width), col_axes[i][:cut], col_axes[i][cut:] + row_axes) for i in range(2)
    ]
    a_plans = [plan(a_part, a_ref, a_acc, (i * width, width), col_axes[i], []) for i in range(2)]
    wide = b_part.shape[1] // 2
    b_plans = [plan(b_part, b_ref, b_acc, (i * wide, wide), order, [])
               for i, order in enumerate((row_axes, row_axes[::-1]))]

    nc, nr = len(col_bits), len(row_bits)
    early = min(2, nr)
    for step in range(len(s_plans[0])):
        for steps in s_plans:
            steps[step][0]()
        if step == 0:
            for steps in b_plans:
                steps[0][0]()
        if step < 2:
            half = prior_ref.shape[0] // TILE // 2
            pick_columns(prior_ref, one_ref, a_part, step * half, (step + 1) * half)
        if nc <= step < nc + early:
            for steps in a_plans:
                steps[step - nc][0]()
        if step == nc + nr:
            for steps in b_plans:
                steps[1][0]()
        for steps in s_plans:
            steps[step][1]()
        if step == nc - 1:
            for steps in b_plans:
                steps[0][1]()
        if nc <= step < nc + early:
            for steps in a_plans:
                steps[step - nc][1]()

    total = TICKS * (obs // NB)
    actions = [[] for _ in range(total + 1)]
    for steps in a_plans:
        left = steps[early:]
        actions[0].append(left[0][0])
        for index in range(len(left)):
            slot = actions[round((total - 1) * (index + 1) / len(left))]
            slot.append(left[index][1])
            slot += [step[0] for step in left[index + 1:index + 2]]
    for steps in b_plans:
        left = steps[1:]
        for index in range(len(left)):
            slot = actions[1 + round((total - 1) * (index / (len(left) - 1)) ** 1.5)]
            slot.append(left[index][1])
            slot += [step[0] for step in left[index + 1:index + 2]]

    i = lax.broadcasted_iota(jnp.int32, (obs, obs), 0)
    j = lax.broadcasted_iota(jnp.int32, (obs, obs), 1)
    sm[:, :obs] = jnp.zeros((obs, obs), F32)
    for (r, n, c, w), (y, x) in packed_blocks(obs):
        sm[y:y + n, x:x + w] = s_ref[r:r + n, c:c + w]
    sm[:, :obs] += jnp.where(i == j, noise_ref[...], 0.0)
    sm[:, obs:] = jnp.where(i == j, 1.0, 0.0)
    eye = jnp.where(i[:NB, :NB] == j[:NB, :NB], 1.0, 0.0).astype(F32)
    wide = lax.broadcasted_iota(jnp.int32, (NB, obs), 1)

    @pl.loop(0, obs // NB)
    def _(kb):
        def tick(mb):
            for block in range(obs // NB):
                todo = actions[block * TICKS + mb]
                if todo:
                    @pl.when(kb == block)
                    def _():
                        for act in todo:
                            act()

        at = pl.ds(pl.multiple_of(kb * NB, NB), NB)
        linv = factor_block(sm[at, at], eye, tick)
        row = jnp.dot(linv, sm[at, :], precision=HI, preferred_element_type=F32)
        inv_ref[at, :] = row[:, obs:]
        below = jnp.where(wide >= (kb + 1) * NB, row[:, :obs], 0.0)
        sm[...] -= lax.dot_general(below, row, (((0,), (0,)), ((), ())), precision=HI, preferred_element_type=F32)

    for act in actions[total]:
        act()


def update_parts(prior, observed, noise, mesh):
    (rows, cols), obs = prior.shape, observed.shape[0]
    col_bits, row_bits = bits(mesh.shape["col"]), bits(mesh.shape["row"])
    nc, nr = len(col_bits), len(row_bits)
    packed = 5 * obs // 8
    cut = halvings(packed, col_bits)
    copies = 2 * (nc + cut + nr) + 2 * 2 * nc + 2 * 2 * nr
    like = jax.ShapeDtypeStruct
    return pl.pallas_call(
        functools.partial(update_kernel, col_bits, row_bits),
        name="update_parts",
        out_shape=(like((obs, obs), F32), like((rows, obs), F32), like((obs, cols), F32)),
        in_specs=[VMEM] * 3,
        out_specs=(VMEM,) * 3,
        scratch_shapes=[
            pltpu.VMEM((packed, obs), F32),
            pltpu.VMEM((rows, obs), F32),
            pltpu.VMEM((obs, cols), F32),
            pltpu.VMEM((cols, obs), BF16),
            pltpu.VMEM((packed, obs), F32),
            pltpu.VMEM((obs, 2 * obs), F32),
            pltpu.VMEM((packed, obs), F32),
            pltpu.VMEM((rows, obs), F32),
            pltpu.VMEM((obs, cols), F32),
        ]
        + recv_shapes(packed, obs // 2, cut, nc - cut + nr) * 2
        + recv_shapes(rows, obs // 2, nc, 0) * 2
        + recv_shapes(obs, cols // 2, nr, 0) * 2
        + [pltpu.SemaphoreType.DMA((copies,)), pltpu.SemaphoreType.DMA((copies,))],
        compiler_params=pltpu.CompilerParams(collective_id=0, has_side_effects=True, vmem_limit_bytes=LIMIT),
    )(prior, observed[None, :], noise[None, :])


def local(mesh, prior, observed, obs_noise):
    linv, a, b = update_parts(prior, observed, obs_noise, mesh)
    v = jnp.dot(linv, b, precision=MID, preferred_element_type=F32)
    y = jnp.dot(linv.T, v, precision=MID, preferred_element_type=F32)
    return prior - jnp.dot(a, y, precision=MID, preferred_element_type=F32)


def solution(mesh):
    return jax.shard_map(
        functools.partial(local, mesh),
        mesh=mesh,
        in_specs=(P("row", "col"), P(), P()),
        out_specs=P("row", "col"),
        check_vma=False,
    )
```

```python
import functools

import jax
import jax.numpy as jnp
from jax import lax
from jax.experimental import pallas as pl
from jax.experimental.pallas import tpu as pltpu
from jax.sharding import PartitionSpec as P

F32 = jnp.float32
BF16 = jnp.bfloat16
HI = lax.Precision.HIGHEST
MID = lax.Precision.HIGH
MESH = pl.DeviceIdType.MESH
VMEM = pl.BlockSpec(memory_space=pltpu.VMEM)
LIMIT = 60 * 1024 * 1024


def parts3(x):
    first = x.astype(BF16)
    rest = x - first.astype(F32)
    second = rest.astype(BF16)
    third = (rest - second.astype(F32)).astype(BF16)
    return first, second, third


def dot(a, b):
    return jnp.dot(a, b, preferred_element_type=F32)


TILE = 256


def pick_rows(prior_ref, obs_ref, one_ref, s_ref, b_ref):
    rows, cols = prior_ref.shape
    obs = obs_ref.shape[1]
    row_start = lax.axis_index("row") * rows
    col_start = lax.axis_index("col") * cols
    in_cols = lax.broadcasted_iota(jnp.int32, (cols, obs), 0) == obs_ref[...] - col_start
    one_ref[...] = jnp.where(in_cols, 1.0, 0.0).astype(BF16)
    tall = jnp.broadcast_to(obs_ref[...].astype(F32), (8, obs)).T[:, :1].astype(jnp.int32)

    @pl.loop(0, rows // TILE)
    def _(t):
        at = pl.ds(pl.multiple_of(t * TILE, TILE), TILE)
        p1, p2, p3 = parts3(prior_ref[at, :])
        left = lax.broadcasted_iota(jnp.int32, (obs, TILE), 1) == tall - (row_start + t * TILE)
        left = jnp.where(left, 1.0, 0.0).astype(BF16)
        got = dot(left, p1) + dot(left, p2) + dot(left, p3)

        @pl.when(t == 0)
        def _():
            b_ref[...] = got

        @pl.when(t > 0)
        def _():
            b_ref[...] += got

    @pl.loop(0, obs // TILE)
    def _(t):
        at = pl.ds(pl.multiple_of(t * TILE, TILE), TILE)
        g1, g2, g3 = parts3(b_ref[at, :])
        pick = one_ref[...]
        s_ref[at, :obs] = dot(g1, pick) + dot(g2, pick) + dot(g3, pick)


def packed_blocks(obs):
    q = obs // 4
    h = q // 2
    return [
        ((0, q, 0, obs), (0, 0)),
        ((q, q, q, obs - q), (q, q)),
        ((q, q, 0, q), (3 * q, 3 * q)),
        ((2 * q, h, 0, 2 * q), (2 * q, 2 * q)),
        ((2 * q, h, 2 * q, 2 * q), (2 * q + h, 2 * q)),
    ]


def halvings(rows, col_bits):
    count = 0
    while count < len(col_bits) and (rows >> (count + 1)) % 8 == 0:
        count += 1
    return count


def pick_columns(prior_ref, one_ref, a_ref, first, last):
    @pl.loop(first, last)
    def _(t):
        at = pl.ds(pl.multiple_of(t * TILE, TILE), TILE)
        p1, p2, p3 = parts3(prior_ref[at, :])
        pick = one_ref[...]
        a_ref[at, :] = dot(p1, pick) + dot(p2, pick) + dot(p3, pick)


def bits(size):
    return list(range(size.bit_length() - 1))


def partner(axis, bit):
    me = lax.axis_index(axis)
    one = (me // (1 << bit)) % 2
    return one, {axis: me + (1 - 2 * one) * (1 << bit)}


def greet(axes):
    barrier = pltpu.get_barrier_semaphore()
    for axis, bit in axes:
        _, peer = partner(axis, bit)
        pl.semaphore_signal(barrier, inc=1, device_id=peer, device_id_type=MESH)
    pl.semaphore_wait(barrier, len(axes))


def phases(src, out, acc, recv, send_sem, recv_sem, first_sem, lanes, halving, whole):
    lane = pl.ds(lanes[0], lanes[1])
    off, n, live = 0, src.shape[0], src
    result, path = [], []

    def at(off, n):
        return pl.ds(pl.multiple_of(off, 8), n)

    def send(source, target, peer):
        sem = first_sem + len(result)
        return pltpu.make_async_remote_copy(
            source, target, send_sem.at[sem], recv_sem.at[sem], device_id=peer, device_id_type=MESH)

    def reducing(copy, where, live, buf):
        def finish():
            copy.wait()
            acc[where, lane] = live[where, lane] + buf[...]

        result.append((copy.start, finish))

    for axis, bit in halving:
        one, peer = partner(axis, bit)
        n //= 2
        give = at(off + (1 - one) * n, n)
        off = off + one * n
        buf = recv[len(result)]
        reducing(send(live.at[give, lane], buf, peer), at(off, n), live, buf)
        live = acc
        path.append((off, n, peer))
    for axis, bit in whole:
        _, peer = partner(axis, bit)
        buf = recv[len(result)]
        where = at(off, n)
        reducing(send(acc.at[where, lane], buf, peer), where, acc, buf)
    for index, (off, n, peer) in enumerate(path[::-1]):
        where = at(off, n)
        copy = send(out.at[where, lane], out.at[where, lane], peer)

        def start(copy=copy, where=where, first=index == 0):
            if first:
                out[where, lane] = acc[where, lane]
            copy.start()

        result.append((start, copy.wait))
    return result


def orders(col_bits):
    return [col_bits, col_bits[:1] + col_bits[1:][::-1]]


def recv_shapes(rows, width, halving, whole):
    shapes = []
    for _ in range(halving):
        rows //= 2
        shapes.append(pltpu.VMEM((rows, width), F32))
    return shapes + [pltpu.VMEM((rows, width), F32)] * whole


def row_of(x, k):
    return jnp.broadcast_to(x[k:k + 1, :], x.shape)


def factor_block(d, m, tick):
    size = d.shape[0]
    tall = size // TICKS
    tiles = tall // 8
    sub = lax.broadcasted_iota(jnp.int32, (8, size), 0)
    done = []
    for hb in range(TICKS):
        tick(hb)
        panel = [d[8 * t:8 * t + 8] for t in range(tiles)]
        right = [m[8 * t:8 * t + 8] for t in range(tiles)]
        for g in range(tiles):
            base = hb * tall + 8 * g
            cols = {
                (t, j): jnp.broadcast_to(panel[t][:, base + j:base + j + 1], (8, size))
                for t in range(g, tiles) for j in range(8)
            }
            for k in range(8):
                lead = cols[g, k]
                inv = lax.rsqrt(row_of(lead, k))
                inv2 = inv * inv
                up, um = row_of(panel[g], k) * inv, row_of(right[g], k) * inv
                ahead = {j: row_of(lead, j) for j in range(k + 1, 8)}
                for t in range(g, tiles):
                    scaled = cols[t, k] * inv2
                    for j in range(k + 1, 8):
                        cols[t, j] = cols[t, j] - scaled * ahead[j]
                    low = cols[t, k] * inv
                    if t == g:
                        low = jnp.where(sub > k, low, 0.0)
                    panel[t] = panel[t] - low * up
                    right[t] = right[t] - low * um
                panel[g] = jnp.where(sub == k, up, panel[g])
                right[g] = jnp.where(sub == k, um, right[g])
        panel, right = jnp.concatenate(panel, axis=0), jnp.concatenate(right, axis=0)
        done.append(right)
        if hb + 1 < TICKS:
            both = jnp.concatenate([panel, right], axis=1)
            step = lax.dot_general(panel, both, (((0,), (0,)), ((), ())), precision=HI, preferred_element_type=F32)
            step = step[tall * (hb + 1):]
            d = d[tall:] - step[:, :size]
            m = m[tall:] - step[:, size:]
    return jnp.concatenate(done, axis=0)


NB = 128
TICKS = 4


def update_kernel(col_bits, row_bits, prior_ref, obs_ref, noise_ref, inv_ref, a_ref, b_ref, s_part, a_part, b_part, one_ref,
                  s_ref, sm, *rest):
    send_sem, recv_sem = rest[-2:]
    obs = obs_ref.shape[1]
    pick_rows(prior_ref, obs_ref, one_ref, sm, b_part)
    for (r, n, c, w), (y, x) in packed_blocks(obs):
        s_part[r:r + n, c:c + w] = sm[y:y + n, x:x + w]
    (s_acc, a_acc, b_acc), bufs = rest[:3], list(rest[3:-2])
    col_axes = [[("col", b) for b in order] for order in orders(col_bits)]
    row_axes = [("row", b) for b in row_bits]
    greet(col_axes[0] + row_axes)
    sems = [0]

    def plan(src, out, acc, lanes, halving, whole):
        count = len(halving) + len(whole)
        mine = [bufs.pop(0) for _ in range(count)]
        steps = phases(src, out, acc, mine, send_sem, recv_sem, sems[0], lanes, halving, whole)
        sems[0] += len(steps)
        return steps

    width = obs // 2
    cut = halvings(s_part.shape[0], col_bits)
    s_plans = [
        plan(s_part, s_ref, s_acc, (i * width, width), col_axes[i][:cut], col_axes[i][cut:] + row_axes) for i in range(2)
    ]
    a_plans = [plan(a_part, a_ref, a_acc, (i * width, width), col_axes[i], []) for i in range(2)]
    wide = b_part.shape[1] // 2
    b_plans = [plan(b_part, b_ref, b_acc, (i * wide, wide), order, [])
               for i, order in enumerate((row_axes, row_axes[::-1]))]

    nc, nr = len(col_bits), len(row_bits)
    early = min(2, nr)
    for step in range(len(s_plans[0])):
        for steps in s_plans:
            steps[step][0]()
        if step == 0:
            for steps in b_plans:
                steps[0][0]()
        if step < 2:
            half = prior_ref.shape[0] // TILE // 2
            pick_columns(prior_ref, one_ref, a_part, step * half, (step + 1) * half)
        if nc <= step < nc + early:
            for steps in a_plans:
                steps[step - nc][0]()
        if step == nc + nr:
            for steps in b_plans:
                steps[1][0]()
        for steps in s_plans:
            steps[step][1]()
        if step == nc:
            for steps in b_plans:
                steps[0][1]()
        if nc <= step < nc + early - 1:
            for steps in a_plans:
                steps[step - nc][1]()

    total = TICKS * (obs // NB)
    actions = [[] for _ in range(total + 1)]
    for steps in a_plans:
        left = steps[early:]
        actions[0] += [steps[early - 1][1], left[0][0]]
        for index in range(len(left)):
            slot = actions[round((total - 1) * (index + 1) / len(left))]
            slot.append(left[index][1])
            slot += [step[0] for step in left[index + 1:index + 2]]
    for steps in b_plans:
        left = steps[1:]
        for index in range(len(left)):
            slot = actions[1 + round((total - 1) * (index / (len(left) - 1)) ** 1.5)]
            slot.append(left[index][1])
            slot += [step[0] for step in left[index + 1:index + 2]]

    i = lax.broadcasted_iota(jnp.int32, (obs, obs), 0)
    j = lax.broadcasted_iota(jnp.int32, (obs, obs), 1)
    sm[:, :obs] = jnp.zeros((obs, obs), F32)
    for (r, n, c, w), (y, x) in packed_blocks(obs):
        sm[y:y + n, x:x + w] = s_ref[r:r + n, c:c + w]
    sm[:, :obs] += jnp.where(i == j, noise_ref[...], 0.0)
    sm[:, obs:] = jnp.where(i == j, 1.0, 0.0)
    eye = jnp.where(i[:NB, :NB] == j[:NB, :NB], 1.0, 0.0).astype(F32)
    wide = lax.broadcasted_iota(jnp.int32, (NB, obs), 1)

    @pl.loop(0, obs // NB)
    def _(kb):
        def tick(mb):
            for block in range(obs // NB):
                todo = actions[block * TICKS + mb]
                if todo:
                    @pl.when(kb == block)
                    def _():
                        for act in todo:
                            act()

        at = pl.ds(pl.multiple_of(kb * NB, NB), NB)
        linv = factor_block(sm[at, at], eye, tick)
        row = jnp.dot(linv, sm[at, :], precision=HI, preferred_element_type=F32)
        inv_ref[at, :] = row[:, obs:]
        below = jnp.where(wide >= (kb + 1) * NB, row[:, :obs], 0.0)
        sm[...] -= lax.dot_general(below, row, (((0,), (0,)), ((), ())), precision=HI, preferred_element_type=F32)

    for act in actions[total]:
        act()


def update_parts(prior, observed, noise, mesh):
    (rows, cols), obs = prior.shape, observed.shape[0]
    col_bits, row_bits = bits(mesh.shape["col"]), bits(mesh.shape["row"])
    nc, nr = len(col_bits), len(row_bits)
    packed = 5 * obs // 8
    cut = halvings(packed, col_bits)
    copies = 2 * (nc + cut + nr) + 2 * 2 * nc + 2 * 2 * nr
    like = jax.ShapeDtypeStruct
    return pl.pallas_call(
        functools.partial(update_kernel, col_bits, row_bits),
        name="update_parts",
        out_shape=(like((obs, obs), F32), like((rows, obs), F32), like((obs, cols), F32)),
        in_specs=[VMEM] * 3,
        out_specs=(VMEM,) * 3,
        scratch_shapes=[
            pltpu.VMEM((packed, obs), F32),
            pltpu.VMEM((rows, obs), F32),
            pltpu.VMEM((obs, cols), F32),
            pltpu.VMEM((cols, obs), BF16),
            pltpu.VMEM((packed, obs), F32),
            pltpu.VMEM((obs, 2 * obs), F32),
            pltpu.VMEM((packed, obs), F32),
            pltpu.VMEM((rows, obs), F32),
            pltpu.VMEM((obs, cols), F32),
        ]
        + recv_shapes(packed, obs // 2, cut, nc - cut + nr) * 2
        + recv_shapes(rows, obs // 2, nc, 0) * 2
        + recv_shapes(obs, cols // 2, nr, 0) * 2
        + [pltpu.SemaphoreType.DMA((copies,)), pltpu.SemaphoreType.DMA((copies,))],
        compiler_params=pltpu.CompilerParams(collective_id=0, has_side_effects=True, vmem_limit_bytes=LIMIT),
    )(prior, observed[None, :], noise[None, :])


def local(mesh, prior, observed, obs_noise):
    linv, a, b = update_parts(prior, observed, obs_noise, mesh)
    v = jnp.dot(linv, b, precision=MID, preferred_element_type=F32)
    y = jnp.dot(linv.T, v, precision=MID, preferred_element_type=F32)
    return prior - jnp.dot(a, y, precision=MID, preferred_element_type=F32)


def solution(mesh):
    return jax.shard_map(
        functools.partial(local, mesh),
        mesh=mesh,
        in_specs=(P("row", "col"), P(), P()),
        out_specs=P("row", "col"),
        check_vma=False,
    )
```
